256 devices in a mesh: sens: 4 (over z_lo, core), par: 64 (over z_hi, x, y).
Axes of the slice: x: 4, y: 4, z: 8 (z_hi: 4, z_lo: 2; z = z_hi * 2 + z_lo), core: 2. Of those that a mesh axis runs over, the one named last changes fastest.
Arguments:
- model: bfloat16 [4, 1024, 256], P('sens', 'par'), may hold values from -6 to 6
- kernel: bfloat16 [512, 1024, 256], P('sens', 'par'), may hold values from -0.01171875 to 0.01171875
- observed: float32 [4, 512, 256], P(None, 'sens'), may hold values from -6 to 6
- weights: float32 [512], P('sens'), may hold values from 0.25 to 4
Outputs:
- gradient: float32 [4, 1024, 256], P('sens', 'par')
- misfit: float32 [], replicated
The draws below stay inside these ranges and needn't reach their ends.
All inputs are finite; a program needn't handle non-finite values.
Results may differ from the reference program's by a relative error of at most 0.0027.
Values may be sent and summed in bfloat16 or wider, within the bound.
A program may use at most 192 MiB of HBM per device.

```python
import math
import jax
import jax.numpy as jnp
from jax import lax

V = 4
S = 512
NT = 256
P_DEV = 16
PARAMETER_TOTAL = 1024
N_PAR = 64


def block_scale(rng, dims, split, low, high):
    level, own = 1.0, jax.random.fold_in(rng, 6)
    for position, shards_of in split:
        draws = jnp.exp(jax.random.uniform(jax.random.fold_in(own, position), (shards_of,), jnp.float32, low / len(split), high / len(split)))
        level = level * jnp.repeat(draws, dims[position] // shards_of).reshape([-1 if axis == position else 1 for axis in range(len(dims))])
    return level


def scatter_about(own_key, extent, width, limit, pieces=(), kind=jnp.bfloat16):
    entries = jax.random.normal(own_key, extent, jnp.float32) * width
    if len(pieces) > 0:
        entries = block_scale(own_key, extent, pieces, -0.22, 0.18) * entries
    return jnp.clip(entries, min=-limit, max=limit).astype(kind)


def setup_inputs(seed: int = 0) -> dict:
    streams_of = jax.random.split(jax.random.key(seed), 5)
    return {
        "model": scatter_about(streams_of[0], (V, PARAMETER_TOTAL, NT), 1.0, 6.0, ((0, 4), (1, 64))),
        "kernel": scatter_about(streams_of[1], (S, PARAMETER_TOTAL, NT), (PARAMETER_TOTAL * NT) ** -0.5, 0.01171875, ((0, 4), (1, 64))),
        "observed": scatter_about(streams_of[2], (V, S, NT), 0.7, 6.0, ((1, 4),), jnp.float32),
        "weights": jnp.clip(jnp.exp(math.log(4.0) - 2.7725887 * jax.random.uniform(streams_of[3], (S,), jnp.float32) ** block_scale(streams_of[3], (S,), ((0, 4),), -0.2, 0.2)), 0.25, 4.0),
    }


def causal_rows(series):
    length_steps = series.shape[-1]
    padded = jnp.concatenate([series, jnp.zeros_like(series)], axis=-1)
    reps = (1,) * (series.ndim - 1) + (length_steps,)
    flat = jnp.tile(padded, reps)
    stride = 2 * length_steps - 1
    flat = flat[..., : length_steps * stride].reshape(series.shape[:-1] + (length_steps, stride))
    return flat[..., :length_steps]


def leading_rows(series):
    length_steps = series.shape[-1]
    padded = jnp.concatenate([series, jnp.zeros_like(series)], axis=-1)
    reps = (1,) * (series.ndim - 1) + (length_steps + 1,)
    flat = jnp.tile(padded, reps)
    stride = 2 * length_steps + 1
    flat = flat[..., : length_steps * stride].reshape(series.shape[:-1] + (length_steps, stride))
    return flat[..., :length_steps]


def reference(model, kernel, observed, weights):
    slabs = kernel.reshape(S, N_PAR, P_DEV, NT).transpose(1, 0, 2, 3)
    model_slabs = model.reshape(V, N_PAR, P_DEV, NT)
    predicted_list = []
    for vector in range(V):
        def forward_step(carry, pair):
            kernel_slab, model_slab = pair
            toeplitz_operator = causal_rows(model_slab.astype(jnp.float32))
            term = jnp.einsum('spk,pkt->st', kernel_slab.astype(jnp.float32), toeplitz_operator)
            return carry + term, None
        summed, _ = lax.scan(forward_step, jnp.zeros((S, NT), jnp.float32), (slabs, model_slabs[vector]))
        predicted_list.append(summed)
    predicted = jnp.stack(predicted_list)
    mismatch = predicted - observed
    weighted_residual = weights[None, :, None] * mismatch
    misfit = 0.5 * jnp.sum(weighted_residual * mismatch) / (V * S * NT)
    residual = weighted_residual.astype(jnp.bfloat16)
    gradient_list = []
    for vector in range(V):
        shifted = leading_rows(residual[vector].astype(jnp.float32))

        def adjoint_slab(kernel_slab):
            return jnp.einsum('spk,skt->pt', kernel_slab.astype(jnp.float32), shifted)
        per_slab = lax.map(adjoint_slab, slabs)
        gradient_list.append(per_slab.reshape(PARAMETER_TOTAL, NT))
    gradient = jnp.stack(gradient_list)
    return gradient, misfit
```

```python
import functools

import jax
import jax.numpy as jnp
from jax import lax
from jax.experimental import pallas as pl
from jax.experimental.pallas import tpu as pltpu
from jax.sharding import PartitionSpec as P

MESH = pl.DeviceIdType.MESH
F32 = jnp.float32
BF16 = jnp.bfloat16
NX = 4
NY = 4
B = 16
ORDER = (2, 1, 3)


def nt(a, b):
    return lax.dot_general(a, b, (((1,), (1,)), ((), ())), preferred_element_type=F32)


def nn(a, b):
    return jnp.dot(a, b, preferred_element_type=F32)


def kernel(
    nz,
    scale,
    model_ref,
    kern_ref,
    obs_ref,
    w_ref,
    grad_ref,
    mis_ref,
    kv,
    kp,
    kt,
    w2,
    eye,
    swap,
    mg,
    xp,
    o0,
    o1,
    ot,
    s0,
    s1,
    r0,
    r1,
    a0,
    a1,
    q0,
    q1,
    zb,
    rf,
    rp,
    mq,
    mr,
    gs,
    gr,
    lsem,
    ssem,
    rsem,
):
    g = lax.axis_index("sens")
    par = lax.axis_index("par")
    z = par // (NX * NY)
    x = (par // NY) % NX
    y = par % NY

    def at_sens(d):
        return {"sens": (g + d) % 4, "par": par}

    def at_x(d):
        return {"sens": g, "par": (z * NX + (x + d) % NX) * NY + y}

    def at_y(d):
        return {"sens": g, "par": (z * NX + x) * NY + (y + d) % NY}

    def at_z(d):
        return {"sens": g, "par": (((z + d) % nz) * NX + x) * NY + y}

    counter = [0]
    pending = []

    def phase():
        base = counter[0]
        counter[0] += 3
        return base

    def send(base, d, src, dst, to):
        c = pltpu.make_async_remote_copy(
            src_ref=src,
            dst_ref=dst,
            send_sem=ssem.at[base + d - 1],
            recv_sem=rsem.at[base + d - 1],
            device_id=to,
            device_id_type=MESH,
        )
        c.start()
        pending.append(c)
        return c

    loads = []
    for n in range(4):
        c = pltpu.make_async_copy(kern_ref.at[pl.ds(512 * n, 512)], kv.at[pl.ds(512 * n, 512)], lsem.at[n])
        c.start()
        loads.append(c)
    own = pltpu.make_async_copy(model_ref.at[0], mg.at[g], lsem.at[4])
    own.start()
    lo0 = pltpu.make_async_copy(obs_ref.at[x, :, pl.ds(0, 128)], o0, lsem.at[5])
    lo0.start()
    lo1 = pltpu.make_async_copy(obs_ref.at[y, :, pl.ds(128, 128)], o1, lsem.at[6])
    lo1.start()

    barrier = pltpu.get_barrier_semaphore()
    zs = tuple(range(1, nz))
    for d in zs:
        pl.semaphore_signal(barrier, inc=1, device_id=at_z(d), device_id_type=MESH)
    for d in ORDER:
        pl.semaphore_signal(barrier, inc=1, device_id=at_x(d), device_id_type=MESH)
        pl.semaphore_signal(barrier, inc=1, device_id=at_y(d), device_id_type=MESH)
        pl.semaphore_signal(barrier, inc=1, device_id=at_sens(d), device_id_type=MESH)

    rows = lax.broadcasted_iota(jnp.int32, (256, 256), 0)
    cols = lax.broadcasted_iota(jnp.int32, (256, 256), 1)
    eye[...] = jnp.where(rows == cols, 1.0, 0.0).astype(BF16)
    swap[...] = jnp.where((rows % 16) * 16 + rows // 16 == cols, 1.0, 0.0).astype(BF16)
    for v in range(4):
        xp[v, 0:240, :] = jnp.zeros((240, 256), BF16)

    for n in range(4):
        loads[n].wait()
        for m in (2 * n, 2 * n + 1):
            out = nn(swap[...], kv[pl.ds(256 * m, 256), :]).astype(BF16)
            kp[:, pl.ds(16 * m, 16), :] = out.reshape(16, 16, 256)

    pl.semaphore_wait(barrier, 9 + len(zs))
    ph = phase()
    gather = [send(ph, d, model_ref.at[0], mg.at[g], at_sens(d)) for d in ORDER]

    for q in range(8):
        out = nt(eye[...], kp[2 * q : 2 * q + 2].reshape(256, 256)).astype(BF16)
        kt[2 * q] = out[:, :128]
        kt[2 * q + 1] = out[:, 128:]
    for c in range(8):
        lo = kt[:, 32 * c : 32 * c + 16, :].reshape(256, 128)
        hi = kt[:, 32 * c + 16 : 32 * c + 32, :].reshape(256, 128)
        out = nn(swap[...], jnp.concatenate([lo, hi], axis=1)).astype(BF16)
        w2[2 * c] = out[:, :128]
        w2[2 * c + 1] = out[:, 128:]

    lo0.wait()
    ot[0] = o0[...].T
    lo1.wait()
    ot[1] = o1[...].T

    own.wait()
    for c in gather:
        c.wait_recv()

    lane = lax.broadcasted_iota(jnp.int32, (16, 256), 1)
    for v in range(4):
        m = mg[v].astype(F32)
        pieces = [m.astype(BF16)]
        for i in range(1, B):
            pieces.append(jnp.where(lane >= i, pltpu.roll(m, i, axis=1), 0.0).astype(BF16))
        stack = jnp.concatenate(pieces, axis=0)
        xp[v, 240:496, :] = nt(eye[...], stack).astype(BF16)

    def predict(v, h):
        blocks = 8 * (h + 1)
        lhs = jnp.concatenate(
            [xp[v, 240 + 128 * h - 16 * a : 368 + 128 * h - 16 * a, :] for a in range(blocks)], axis=1
        )
        return nn(lhs, w2[0:blocks].reshape(blocks * 256, 128))

    ph0 = phase()
    ph1 = phase()
    in0, in1 = {}, {}
    for d in ORDER:
        s1[d] = predict((y + d) % NY, 1)
        in1[d] = send(ph1, d, s1.at[d], r1.at[d - 1], at_y(d))
        s0[d] = predict((x + d) % NX, 0)
        in0[d] = send(ph0, d, s0.at[d], r0.at[d - 1], at_x(d))
    s1[0] = predict(y, 1)
    s0[0] = predict(x, 0)

    ph2 = phase()
    ph3 = phase()
    for d in ORDER:
        in0[d].wait_recv()
    a0[...] = (s0[0] + r0[0]) + (r0[1] + r0[2])
    in2 = {}
    for d in ORDER:
        rows32 = pl.ds(pl.multiple_of(32 * ((y + d) % NY), 32), 32)
        in2[d] = send(ph2, d, a0.at[rows32], q0.at[d - 1], at_y(d))
    for d in ORDER:
        in1[d].wait_recv()
    a1[...] = (s1[0] + r1[0]) + (r1[1] + r1[2])
    in3 = {}
    for d in ORDER:
        rows32 = pl.ds(pl.multiple_of(32 * ((x + d) % NX), 32), 32)
        in3[d] = send(ph3, d, a1.at[rows32], q1.at[d - 1], at_x(d))

    my = pl.ds(pl.multiple_of(32 * y, 32), 32)
    mx = pl.ds(pl.multiple_of(32 * x, 32), 32)
    ph4 = phase()
    ph5 = phase()
    for d in ORDER:
        in2[d].wait_recv()
    zb[0, z] = (a0[my, :] + q0[0]) + (q0[1] + q0[2])
    in4 = [send(ph4, d, zb.at[0, z], zb.at[0, z], at_z(d)) for d in zs]
    for d in ORDER:
        in3[d].wait_recv()
    zb[1, z] = (a1[mx, :] + q1[0]) + (q1[1] + q1[2])
    in5 = [send(ph5, d, zb.at[1, z], zb.at[1, z], at_z(d)) for d in zs]

    weights = w_ref[...]

    def settle(h, rows32):
        total = zb[h, 0]
        for n in range(1, nz):
            total = total + zb[h, n]
        mismatch = total - ot[h, rows32, :]
        weighted = weights * mismatch
        sq = (weighted * mismatch).reshape(4, 8, 128)
        return weighted.astype(BF16), (sq[0] + sq[1]) + (sq[2] + sq[3])

    ph6 = phase()
    ph7 = phase()
    phq = phase()
    for c in in4:
        c.wait_recv()
    res, sq0 = settle(0, my)
    rf[x, my, :] = res
    in6 = [send(ph6, d, rf.at[x, my], rf.at[x, my], at_y(d)) for d in ORDER]
    for c in in5:
        c.wait_recv()
    res, sq1 = settle(1, mx)
    mx1 = pl.ds(pl.multiple_of(128 + 32 * x, 32), 32)
    rf[y, mx1, :] = res
    in7 = [send(ph7, d, rf.at[y, mx1], rf.at[y, mx1], at_x(d)) for d in ORDER]
    mq[0] = sq0 + sq1
    inq = [send(phq, d, mq.at[0], mr.at[y], at_y(d)) for d in ORDER]
    mr[y] = sq0 + sq1

    ph8 = phase()
    ph9 = phase()
    phr = phase()
    for c in in6:
        c.wait_recv()
    in8 = [send(ph8, d, rf.at[x, 0:128], rf.at[x, 0:128], at_x(d)) for d in ORDER]
    for c in in7:
        c.wait_recv()
    in9 = [send(ph9, d, rf.at[y, 128:256], rf.at[y, 128:256], at_y(d)) for d in ORDER]
    for c in inq:
        c.wait_recv()
    sq = (mr[0] + mr[1]) + (mr[2] + mr[3])
    mq[1] = sq
    inr = [send(phr, d, mq.at[1], mr.at[4 + x], at_x(d)) for d in ORDER]
    mr[4 + x] = sq
    for c in in8 + in9 + inr:
        c.wait_recv()
    sq = (mr[4] + mr[5]) + (mr[6] + mr[7])

    rp[256:272, :] = jnp.zeros((16, 128), F32)

    def adjoint(v):
        rp[0:256, :] = rf[v].astype(F32)
        lhs = jnp.concatenate([rp[i : i + 256, :].astype(BF16) for i in range(B)], axis=1)
        rhs = jnp.concatenate([w2[:, 16 * i : 16 * i + 16, :].reshape(256, 128) for i in range(B)], axis=1)
        out = nt(lhs, rhs)
        total = out[:, :128] + jnp.concatenate([out[128:, 128:], jnp.zeros((128, 128), F32)], axis=0)
        for lanes in (64, 32, 16):
            moved = pltpu.roll(total, 128 - lanes, axis=1)
            total = total + jnp.concatenate([moved[lanes:], jnp.zeros((lanes, 128), F32)], axis=0)
        low = lax.broadcasted_iota(jnp.int32, (32, 128), 1) < 16
        packed = jnp.where(low, total[0:32], 0.0)
        for c in range(1, 8):
            packed = packed + pltpu.roll(jnp.where(low, total[32 * c : 32 * c + 32], 0.0), 16 * c, axis=1)
        return packed

    phg = phase()
    ing = {}
    for d in ORDER:
        gs[d, 0:32, :] = adjoint((g + d) % 4)
        gs[d, 32:40, :] = sq
        ing[d] = send(phg, d, gs.at[d], gr.at[d - 1], at_sens(d))
    mine = adjoint(g)
    for d in ORDER:
        ing[d].wait_recv()
    grad_ref[...] = (mine + gr[0, 0:32]) + (gr[1, 0:32] + gr[2, 0:32])
    total = jnp.zeros((8, 128), F32)
    parts = [sq] + [gr[d - 1, 32:40] for d in (1, 2, 3)]
    for owner in range(4):
        for d in range(4):
            total = total + jnp.where((g + 4 - d) % 4 == owner, parts[d], 0.0)
    mis_ref[...] = jnp.broadcast_to(jnp.sum(total, keepdims=True) * scale, (8, 128))
    for c in pending:
        c.wait_send()


def local(nz, scale, model, kern, observed, weights):
    sems = 60
    grad, mis = pl.pallas_call(
        functools.partial(kernel, nz, scale),
        out_shape=(jax.ShapeDtypeStruct((32, 128), F32), jax.ShapeDtypeStruct((8, 128), F32)),
        in_specs=[pl.BlockSpec(memory_space=pl.ANY)] * 3 + [pl.BlockSpec(memory_space=pltpu.VMEM)],
        out_specs=(pl.BlockSpec(memory_space=pltpu.VMEM),) * 2,
        scratch_shapes=[
            pltpu.VMEM((2048, 256), BF16),
            pltpu.VMEM((16, 128, 256), BF16),
            pltpu.VMEM((16, 256, 128), BF16),
            pltpu.VMEM((16, 256, 128), BF16),
            pltpu.VMEM((256, 256), BF16),
            pltpu.VMEM((256, 256), BF16),
            pltpu.VMEM((4, 16, 256), BF16),
            pltpu.VMEM((4, 496, 256), BF16),
            pltpu.VMEM((128, 128), F32),
            pltpu.VMEM((128, 128), F32),
            pltpu.VMEM((2, 128, 128), F32),
            pltpu.VMEM((4, 128, 128), F32),
            pltpu.VMEM((4, 128, 128), F32),
            pltpu.VMEM((3, 128, 128), F32),
            pltpu.VMEM((3, 128, 128), F32),
            pltpu.VMEM((128, 128), F32),
            pltpu.VMEM((128, 128), F32),
            pltpu.VMEM((3, 32, 128), F32),
            pltpu.VMEM((3, 32, 128), F32),
            pltpu.VMEM((2, nz, 32, 128), F32),
            pltpu.VMEM((4, 256, 128), BF16),
            pltpu.VMEM((272, 128), F32),
            pltpu.VMEM((2, 8, 128), F32),
            pltpu.VMEM((8, 8, 128), F32),
            pltpu.VMEM((4, 40, 128), F32),
            pltpu.VMEM((3, 40, 128), F32),
            pltpu.SemaphoreType.DMA((7,)),
            pltpu.SemaphoreType.DMA((sems,)),
            pltpu.SemaphoreType.DMA((sems,)),
        ],
        compiler_params=pltpu.CompilerParams(collective_id=0, has_side_effects=True),
        name="misfit_adjoint",
    )(model, kern.reshape(2048, 256), observed, weights.reshape(1, 128))
    gradient = grad.reshape(32, 8, 16).transpose(2, 1, 0).reshape(1, 16, 256)
    return gradient, mis[0, 0]


def solution(mesh):
    nz = mesh.shape["par"] // (NX * NY)
    entries = 4 * 128 * mesh.shape["sens"] * 256
    return jax.shard_map(
        functools.partial(local, nz, 0.5 / entries),
        mesh=mesh,
        in_specs=(P("sens", "par", None), P("sens", "par", None), P(None, "sens", None), P("sens")),
        out_specs=(P("sens", "par", None), P()),
        check_vma=False,
    )
```

```python
import functools

import jax
import jax.numpy as jnp
from jax import lax
from jax.experimental import pallas as pl
from jax.experimental.pallas import tpu as pltpu
from jax.sharding import PartitionSpec as P

MESH = pl.DeviceIdType.MESH
F32 = jnp.float32
BF16 = jnp.bfloat16
NX = 4
NY = 4
B = 16
ORDER = (2, 1, 3)
PLANE = tuple((dx, dy) for dx in (2, 1, 3, 0) for dy in (2, 1, 3, 0) if dx or dy)


def nt(a, b):
    return lax.dot_general(a, b, (((1,), (1,)), ((), ())), preferred_element_type=F32)


def nn(a, b):
    return jnp.dot(a, b, preferred_element_type=F32)


def kernel(
    nz,
    scale,
    model_ref,
    kern_ref,
    obs_ref,
    weights_ref,
    out_ref,
    kv,
    kp,
    kt,
    w2,
    eye,
    swap,
    w_ref,
    mg,
    xp,
    ob,
    ot,
    sp,
    rs,
    zb,
    rf,
    rp,
    mq,
    mr,
    gs,
    gr,
    lsem,
    ssem,
    rsem,
):
    g = lax.axis_index("sens")
    par = lax.axis_index("par")
    z = par // (NX * NY)
    x = (par // NY) % NX
    y = par % NY

    def at_sens(d):
        return {"sens": (g + d) % 4, "par": par}

    def at_plane(dx, dy):
        return {"sens": g, "par": (z * NX + (x + dx) % NX) * NY + (y + dy) % NY}

    def at_z(d):
        return {"sens": g, "par": (((z + d) % nz) * NX + x) * NY + y}

    counter = [0]
    pending = []

    def phase(copies=3):
        base = counter[0]
        counter[0] += copies
        return base

    def send(number, src, dst, to):
        c = pltpu.make_async_remote_copy(
            src_ref=src,
            dst_ref=dst,
            send_sem=ssem.at[number],
            recv_sem=rsem.at[number],
            device_id=to,
            device_id_type=MESH,
        )
        c.start()
        pending.append(c)
        return c

    own = pltpu.make_async_copy(model_ref.at[0], mg.at[g], lsem.at[4])
    own.start()
    loads = []
    for n in range(4):
        c = pltpu.make_async_copy(kern_ref.at[pl.ds(512 * n, 512)], kv.at[pl.ds(512 * n, 512)], lsem.at[n])
        c.start()
        loads.append(c)
    load = pltpu.make_async_copy(
        obs_ref.at[x, :, pl.ds(pl.multiple_of(128 * (y // 2), 128), 128)], ob, lsem.at[5]
    )
    load.start()
    wload = pltpu.make_async_copy(weights_ref, w_ref, lsem.at[6])
    wload.start()

    barrier = pltpu.get_barrier_semaphore()
    zs = tuple(range(1, nz))
    for d in zs:
        pl.semaphore_signal(barrier, inc=1, device_id=at_z(d), device_id_type=MESH)
    for dx, dy in PLANE:
        pl.semaphore_signal(barrier, inc=1, device_id=at_plane(dx, dy), device_id_type=MESH)
    for d in ORDER:
        pl.semaphore_signal(barrier, inc=1, device_id=at_sens(d), device_id_type=MESH)

    rows = lax.broadcasted_iota(jnp.int32, (256, 256), 0)
    cols = lax.broadcasted_iota(jnp.int32, (256, 256), 1)
    eye[...] = jnp.where(rows == cols, 1.0, 0.0).astype(BF16)
    swap[...] = jnp.where((rows % 16) * 16 + rows // 16 == cols, 1.0, 0.0).astype(BF16)

    own.wait()
    pl.semaphore_wait(barrier, len(PLANE) + 3 + len(zs))
    ph = phase()
    gather = [send(ph + d - 1, mg.at[g], mg.at[g], at_sens(d)) for d in ORDER]

    for n in range(4):
        loads[n].wait()
        for m in (2 * n, 2 * n + 1):
            out = nn(swap[...], kv[pl.ds(256 * m, 256), :]).astype(BF16)
            kp[:, pl.ds(16 * m, 16), :] = out.reshape(16, 16, 256)

    for q in range(8):
        out = nt(eye[...], kp[2 * q : 2 * q + 2].reshape(256, 256)).astype(BF16)
        kt[2 * q] = out[:, :128]
        kt[2 * q + 1] = out[:, 128:]
    for c in range(8):
        lo = kt[:, 32 * c : 32 * c + 16, :].reshape(256, 128)
        hi = kt[:, 32 * c + 16 : 32 * c + 32, :].reshape(256, 128)
        out = nn(swap[...], jnp.concatenate([lo, hi], axis=1)).astype(BF16)
        w2[c] = out

    load.wait()
    wload.wait()
    ot[...] = ob[...].T

    for c in gather:
        c.wait_recv()

    lane = lax.broadcasted_iota(jnp.int32, (16, 256), 1)
    for v in range(4):
        m = mg[v].astype(F32)
        pieces = [m.astype(BF16)]
        for i in range(1, B):
            pieces.append(jnp.where(lane >= i, pltpu.roll(m, i, axis=1), 0.0).astype(BF16))
        stack = jnp.concatenate(pieces, axis=0)
        xp[v] = nt(eye[...], stack).astype(BF16)

    def predict(v):
        blocks = [None] * 16
        for c in range(8):
            out = nn(xp[v, 0 : B * (16 - 2 * c), :], w2[c])
            for b in range(16 - 2 * c):
                for e in (0, 1):
                    t = b + 2 * c + e
                    if t < 16:
                        part = out[B * b : B * b + B, 128 * e : 128 * e + 128]
                        blocks[t] = part if blocks[t] is None else blocks[t] + part
        return jnp.concatenate(blocks, axis=0)

    def quarter(n):
        return pl.ds(pl.multiple_of(64 * n, 64), 64)

    pha = phase(len(PLANE))
    ina = {}
    for dx in (2, 1, 3, 0):
        sp[dx] = predict((x + dx) % NX)
        for n, (px, dy) in enumerate(PLANE):
            if px == dx:
                ina[px, dy] = send(pha + n, sp.at[dx, quarter((y + dy) % NY)], rs.at[n], at_plane(dx, dy))
    block = sp[0, quarter(y), :]
    for first in (0, 4, 8, 12):
        group = range(first, min(first + 4, len(PLANE)))
        for n in group:
            ina[PLANE[n]].wait_recv()
        part = rs[first]
        for n in group[1:]:
            part = part + rs[n]
        block = block + part

    phz = phase()
    zb[z] = block
    inz = [send(phz + d - 1, zb.at[z], zb.at[z], at_z(d)) for d in zs]
    for c in inz:
        c.wait_recv()
    total = zb[0]
    for n in range(1, nz):
        total = total + zb[n]

    mismatch = total - ot[pl.ds(pl.multiple_of(64 * (y % 2), 64), 64), :]
    weighted = w_ref[...] * mismatch
    rf[x, quarter(y), :] = weighted.astype(BF16)
    phb = phase(len(PLANE))
    inb = {}
    for n, (dx, dy) in enumerate(PLANE):
        inb[dx, dy] = send(phb + n, rf.at[x, quarter(y)], rf.at[x, quarter(y)], at_plane(dx, dy))

    phy = phase()
    phx = phase()
    sq = (weighted * mismatch).reshape(8, 8, 128)
    sq = ((sq[0] + sq[1]) + (sq[2] + sq[3])) + ((sq[4] + sq[5]) + (sq[6] + sq[7]))
    mq[0] = sq
    mr[y] = sq
    iny = [send(phy + d - 1, mq.at[0], mr.at[y], at_plane(0, d)) for d in ORDER]

    rp[256:272, :] = jnp.zeros((16, 128), F32)
    group = lax.broadcasted_iota(jnp.int32, (B, 128), 1) // B

    def adjoint(v):
        rp[0:256, :] = rf[v].astype(F32)
        lhs = jnp.concatenate([rp[i : i + 256, :].astype(BF16) for i in range(B)], axis=1)
        rhs = jnp.concatenate(
            [
                jnp.concatenate([w2[:, B * i : B * i + B, 0:128], w2[:, B * i : B * i + B, 128:256]], axis=0).reshape(
                    256, 128
                )
                for i in range(B)
            ],
            axis=1,
        )
        out = nt(lhs, rhs)
        t = [out[B * b : B * b + B, :128] for b in range(16)]
        for b in range(15):
            t[b] = t[b] + out[B * b + B : B * b + 2 * B, 128:]
        for half in (0, 1):
            packed = None
            for r in range(-7, 8):
                picked = jnp.zeros((B, 128), F32)
                for c in range(max(0, -r), 8):
                    if 0 <= 2 * c + r < 8:
                        picked = jnp.where(group == c, t[2 * (2 * c + r) + half], picked)
                if r:
                    picked = pltpu.roll(picked, (B * r) % 128, axis=1)
                packed = picked if packed is None else packed + picked
            gs[v, B * half : B * half + B, :] = packed

    for dx in (0, 1, 3, 2):
        for dy in (0, 1, 3, 2):
            if (dx, dy) in inb:
                inb[dx, dy].wait_recv()
        adjoint((x + 4 - dx) % 4)
        if dx == 0:
            for c in iny:
                c.wait_recv()
            sq = (mr[0] + mr[1]) + (mr[2] + mr[3])
            mq[1] = sq
            mr[4 + x] = sq
            inx = [send(phx + d - 1, mq.at[1], mr.at[4 + x], at_plane(d, 0)) for d in ORDER]
    for c in inx:
        c.wait_recv()
    sq = (mr[4] + mr[5]) + (mr[6] + mr[7])

    phg = phase()
    ing = {}
    for d in ORDER:
        v = (g + d) % 4
        gs[v, 32:40, :] = sq
        ing[d] = send(phg + d - 1, gs.at[v], gr.at[d - 1], at_sens(d))
    for d in ORDER:
        ing[d].wait_recv()
    out_ref[0:32, :] = (gs[g, 0:32, :] + gr[0, 0:32]) + (gr[1, 0:32] + gr[2, 0:32])
    total = jnp.zeros((8, 128), F32)
    parts = [sq] + [gr[d - 1, 32:40] for d in (1, 2, 3)]
    for owner in range(4):
        for d in range(4):
            total = total + jnp.where((g + 4 - d) % 4 == owner, parts[d], 0.0)
    out_ref[32:40, :] = total * scale
    for c in pending:
        c.wait_send()


def finish(in_ref, grad_ref, mis_ref):
    series = in_ref[0:32, :].T
    for c in range(8):
        grad_ref[0, :, 32 * c : 32 * c + 32] = series[B * c : B * c + B, :]
    mis_ref[0, 0] = jnp.sum(in_ref[32:40, :])


def local(nz, scale, model, kern, observed, weights):
    sems = 45
    out = pl.pallas_call(
        functools.partial(kernel, nz, scale),
        out_shape=jax.ShapeDtypeStruct((40, 128), F32),
        in_specs=[pl.BlockSpec(memory_space=pltpu.HBM)] * 4,
        out_specs=pl.BlockSpec(memory_space=pltpu.VMEM),
        scratch_shapes=[
            pltpu.VMEM((2048, 256), BF16),
            pltpu.VMEM((16, 128, 256), BF16),
            pltpu.VMEM((16, 256, 128), BF16),
            pltpu.VMEM((8, 256, 256), BF16),
            pltpu.VMEM((256, 256), BF16),
            pltpu.VMEM((256, 256), BF16),
            pltpu.VMEM((1, 128), F32),
            pltpu.VMEM((4, 16, 256), BF16),
            pltpu.VMEM((4, 256, 256), BF16),
            pltpu.VMEM((128, 128), F32),
            pltpu.VMEM((128, 128), F32),
            pltpu.VMEM((4, 256, 128), F32),
            pltpu.VMEM((15, 64, 128), F32),
            pltpu.VMEM((nz, 64, 128), F32),
            pltpu.VMEM((4, 256, 128), BF16),
            pltpu.VMEM((272, 128), F32),
            pltpu.VMEM((2, 8, 128), F32),
            pltpu.VMEM((8, 8, 128), F32),
            pltpu.VMEM((4, 40, 128), F32),
            pltpu.VMEM((3, 40, 128), F32),
            pltpu.SemaphoreType.DMA((7,)),
            pltpu.SemaphoreType.DMA((sems,)),
            pltpu.SemaphoreType.DMA((sems,)),
        ],
        compiler_params=pltpu.CompilerParams(
            collective_id=0, has_side_effects=True, vmem_limit_bytes=24 * 1024 * 1024
        ),
        name="misfit_adjoint",
    )(*[pltpu.with_memory_space_constraint(a, pltpu.HBM) for a in (model, kern.reshape(2048, 256), observed, weights.reshape(1, 128))])
    gradient, misfit = pl.pallas_call(
        finish,
        out_shape=(jax.ShapeDtypeStruct((1, 16, 256), F32), jax.ShapeDtypeStruct((1, 1), F32)),
        in_specs=[pl.BlockSpec(memory_space=pltpu.VMEM)],
        out_specs=(pl.BlockSpec(memory_space=pltpu.VMEM), pl.BlockSpec(memory_space=pltpu.SMEM)),
        compiler_params=pltpu.CompilerParams(vmem_limit_bytes=4 * 1024 * 1024),
        name="finish",
    )(out)
    return gradient, misfit.reshape(())


def solution(mesh):
    nz = mesh.shape["par"] // (NX * NY)
    entries = 4 * 128 * mesh.shape["sens"] * 256
    return jax.shard_map(
        functools.partial(local, nz, 0.5 / entries),
        mesh=mesh,
        in_specs=(P("sens", "par", None), P("sens", "par", None), P(None, "sens", None), P("sens")),
        out_specs=(P("sens", "par", None), P()),
        check_vma=False,
    )
```

```python
import functools

import jax
import jax.numpy as jnp
from jax import lax
from jax.experimental import pallas as pl
from jax.experimental.pallas import tpu as pltpu
from jax.sharding import PartitionSpec as P

MESH = pl.DeviceIdType.MESH
F32 = jnp.float32
BF16 = jnp.bfloat16
NX = 4
NY = 4
B = 16
ORDER = (2, 1, 3)
PLANE = tuple((dx, dy) for dx in (2, 1, 3, 0) for dy in (2, 1, 3, 0) if dx or dy)


def nt(a, b):
    return lax.dot_general(a, b, (((1,), (1,)), ((), ())), preferred_element_type=F32)


def nn(a, b):
    return jnp.dot(a, b, preferred_element_type=F32)


def kernel(
    nz,
    scale,
    model_ref,
    kern_ref,
    obs_ref,
    weights_ref,
    out_ref,
    kv,
    kp,
    kt,
    w2,
    eye,
    swap,
    w_ref,
    mg,
    xp,
    ob,
    ot,
    sp,
    rs,
    zb,
    rf,
    rp,
    mr,
    gs,
    gr,
    lsem,
    ssem,
    rsem,
):
    g = lax.axis_index("sens")
    par = lax.axis_index("par")
    z = par // (NX * NY)
    x = (par // NY) % NX
    y = par % NY

    def at_sens(d):
        return {"sens": (g + d) % 4, "par": par}

    def at_plane(dx, dy):
        return {"sens": g, "par": (z * NX + (x + dx) % NX) * NY + (y + dy) % NY}

    def at_z(d):
        return {"sens": g, "par": (((z + d) % nz) * NX + x) * NY + y}

    counter = [0]
    pending = []

    def phase(copies=3):
        base = counter[0]
        counter[0] += copies
        return base

    def send(number, src, dst, to):
        c = pltpu.make_async_remote_copy(
            src_ref=src,
            dst_ref=dst,
            send_sem=ssem.at[number],
            recv_sem=rsem.at[number],
            device_id=to,
            device_id_type=MESH,
        )
        c.start()
        pending.append(c)
        return c

    own = pltpu.make_async_copy(model_ref.at[0], mg.at[g], lsem.at[4])
    own.start()
    loads = []
    for n in range(4):
        c = pltpu.make_async_copy(kern_ref.at[pl.ds(512 * n, 512)], kv.at[pl.ds(512 * n, 512)], lsem.at[n])
        c.start()
        loads.append(c)
    load = pltpu.make_async_copy(
        obs_ref.at[x, :, pl.ds(pl.multiple_of(128 * (y // 2), 128), 128)], ob, lsem.at[5]
    )
    load.start()
    wload = pltpu.make_async_copy(weights_ref, w_ref, lsem.at[6])
    wload.start()

    barrier = pltpu.get_barrier_semaphore()
    zs = tuple(range(1, nz))
    for d in zs:
        pl.semaphore_signal(barrier, inc=1, device_id=at_z(d), device_id_type=MESH)
    for dx, dy in PLANE:
        pl.semaphore_signal(barrier, inc=1, device_id=at_plane(dx, dy), device_id_type=MESH)
    for d in ORDER:
        pl.semaphore_signal(barrier, inc=1, device_id=at_sens(d), device_id_type=MESH)

    rows = lax.broadcasted_iota(jnp.int32, (256, 256), 0)
    cols = lax.broadcasted_iota(jnp.int32, (256, 256), 1)
    eye[...] = jnp.where(rows == cols, 1.0, 0.0).astype(BF16)
    swap[...] = jnp.where((rows % 16) * 16 + rows // 16 == cols, 1.0, 0.0).astype(BF16)

    own.wait()
    pl.semaphore_wait(barrier, len(PLANE) + 3 + len(zs))
    ph = phase()
    gather = [send(ph + d - 1, mg.at[g], mg.at[g], at_sens(d)) for d in ORDER]

    for n in range(4):
        loads[n].wait()
        for m in (2 * n, 2 * n + 1):
            out = nn(swap[...], kv[pl.ds(256 * m, 256), :]).astype(BF16)
            kp[:, pl.ds(16 * m, 16), :] = out.reshape(16, 16, 256)

    for q in range(8):
        out = nt(eye[...], kp[2 * q : 2 * q + 2].reshape(256, 256)).astype(BF16)
        kt[2 * q] = out[:, :128]
        kt[2 * q + 1] = out[:, 128:]
    for c in range(8):
        lo = kt[:, 32 * c : 32 * c + 16, :].reshape(256, 128)
        hi = kt[:, 32 * c + 16 : 32 * c + 32, :].reshape(256, 128)
        out = nn(swap[...], jnp.concatenate([lo, hi], axis=1)).astype(BF16)
        w2[c] = out

    load.wait()
    wload.wait()
    ot[...] = ob[...].T

    for c in gather:
        c.wait_recv()

    lane = lax.broadcasted_iota(jnp.int32, (16, 256), 1)
    for v in range(4):
        m = mg[v].astype(F32)
        pieces = [m.astype(BF16)]
        for i in range(1, B):
            pieces.append(jnp.where(lane >= i, pltpu.roll(m, i, axis=1), 0.0).astype(BF16))
        stack = jnp.concatenate(pieces, axis=0)
        xp[v] = nt(eye[...], stack).astype(BF16)

    def predict(v):
        blocks = [None] * 16
        for c in range(8):
            out = nn(xp[v, 0 : B * (16 - 2 * c), :], w2[c])
            for b in range(16 - 2 * c):
                for e in (0, 1):
                    t = b + 2 * c + e
                    if t < 16:
                        part = out[B * b : B * b + B, 128 * e : 128 * e + 128]
                        blocks[t] = part if blocks[t] is None else blocks[t] + part
        return jnp.concatenate(blocks, axis=0)

    def quarter(n):
        return pl.ds(pl.multiple_of(64 * n, 64), 64)

    pha = phase(len(PLANE))
    ina = {}
    for some in ((2, 1), (3, 0)):
        for dx in some:
            sp[dx] = predict((x + dx) % NX)
        for n, (px, dy) in enumerate(PLANE):
            if px in some:
                ina[px, dy] = send(pha + n, sp.at[px, quarter((y + dy) % NY)], rs.at[n], at_plane(px, dy))
    block = sp[0, quarter(y), :]
    for first in (0, 4, 8, 12):
        group = range(first, min(first + 4, len(PLANE)))
        for n in group:
            ina[PLANE[n]].wait_recv()
        part = rs[first]
        for n in group[1:]:
            part = part + rs[n]
        block = block + part

    phz = phase()
    zb[z] = block
    inz = [send(phz + d - 1, zb.at[z], zb.at[z], at_z(d)) for d in zs]
    for c in inz:
        c.wait_recv()
    total = zb[0]
    for n in range(1, nz):
        total = total + zb[n]

    mismatch = total - ot[pl.ds(pl.multiple_of(64 * (y % 2), 64), 64), :]
    weighted = w_ref[...] * mismatch
    rf[x, quarter(y), :] = weighted.astype(BF16)
    phb = phase(len(PLANE))
    inb = {}
    for n, (dx, dy) in enumerate(PLANE):
        inb[dx, dy] = send(phb + n, rf.at[x, quarter(y)], rf.at[x, quarter(y)], at_plane(dx, dy))

    sq = jnp.sum((weighted * mismatch).reshape(8, 8, 128), axis=0)
    here = NY * x + y
    mr[here] = jnp.sum(sq, axis=0, keepdims=True)
    phm = phase(len(PLANE))
    inm = [send(phm + n, mr.at[here], mr.at[here], at_plane(dx, dy)) for n, (dx, dy) in enumerate(PLANE)]

    rp[256:272, :] = jnp.zeros((16, 128), F32)
    group = lax.broadcasted_iota(jnp.int32, (B, 128), 1) // B

    def adjoint(v):
        rp[0:256, :] = rf[v].astype(F32)
        lhs = jnp.concatenate([rp[i : i + 256, :].astype(BF16) for i in range(B)], axis=1)
        rhs = jnp.concatenate(
            [
                jnp.concatenate([w2[:, B * i : B * i + B, 0:128], w2[:, B * i : B * i + B, 128:256]], axis=0).reshape(
                    256, 128
                )
                for i in range(B)
            ],
            axis=1,
        )
        out = nt(lhs, rhs)
        t = [out[B * b : B * b + B, :128] for b in range(16)]
        for b in range(15):
            t[b] = t[b] + out[B * b + B : B * b + 2 * B, 128:]
        for half in (0, 1):
            packed = None
            for r in range(-7, 8):
                picked = jnp.zeros((B, 128), F32)
                for c in range(max(0, -r), 8):
                    if 0 <= 2 * c + r < 8:
                        picked = jnp.where(group == c, t[2 * (2 * c + r) + half], picked)
                if r:
                    picked = pltpu.roll(picked, (B * r) % 128, axis=1)
                packed = picked if packed is None else packed + picked
            gs[v, B * half : B * half + B, :] = packed

    for c in inb.values():
        c.wait_recv()
    for v in range(4):
        adjoint(v)
    for c in inm:
        c.wait_recv()
    parts = [mr[n] for n in range(NX * NY)]
    while len(parts) > 1:
        parts = [parts[n] + parts[n + 1] for n in range(0, len(parts), 2)]
    sq = jnp.where(lax.broadcasted_iota(jnp.int32, (8, 128), 0) == 0, parts[0], 0.0)

    phg = phase()
    ing = {}
    for d in ORDER:
        v = (g + d) % 4
        gs[v, 32:40, :] = sq
        ing[d] = send(phg + d - 1, gs.at[v], gr.at[d - 1], at_sens(d))
    for d in ORDER:
        ing[d].wait_recv()
    out_ref[0:32, :] = (gs[g, 0:32, :] + gr[0, 0:32]) + (gr[1, 0:32] + gr[2, 0:32])
    total = jnp.zeros((8, 128), F32)
    parts = [sq] + [gr[d - 1, 32:40] for d in (1, 2, 3)]
    for owner in range(4):
        for d in range(4):
            total = total + jnp.where((g + 4 - d) % 4 == owner, parts[d], 0.0)
    out_ref[32:40, :] = total * scale
    for c in pending:
        c.wait_send()


def finish(in_ref, grad_ref, mis_ref):
    series = in_ref[0:32, :].T
    for c in range(8):
        grad_ref[0, :, 32 * c : 32 * c + 32] = series[B * c : B * c + B, :]
    mis_ref[0, 0] = jnp.sum(in_ref[32:40, :])


def local(nz, scale, model, kern, observed, weights):
    sems = 54
    out = pl.pallas_call(
        functools.partial(kernel, nz, scale),
        out_shape=jax.ShapeDtypeStruct((40, 128), F32),
        in_specs=[pl.BlockSpec(memory_space=pltpu.HBM)] * 4,
        out_specs=pl.BlockSpec(memory_space=pltpu.VMEM),
        scratch_shapes=[
            pltpu.VMEM((2048, 256), BF16),
            pltpu.VMEM((16, 128, 256), BF16),
            pltpu.VMEM((16, 256, 128), BF16),
            pltpu.VMEM((8, 256, 256), BF16),
            pltpu.VMEM((256, 256), BF16),
            pltpu.VMEM((256, 256), BF16),
            pltpu.VMEM((1, 128), F32),
            pltpu.VMEM((4, 16, 256), BF16),
            pltpu.VMEM((4, 256, 256), BF16),
            pltpu.VMEM((128, 128), F32),
            pltpu.VMEM((128, 128), F32),
            pltpu.VMEM((4, 256, 128), F32),
            pltpu.VMEM((15, 64, 128), F32),
            pltpu.VMEM((nz, 64, 128), F32),
            pltpu.VMEM((4, 256, 128), BF16),
            pltpu.VMEM((272, 128), F32),
            pltpu.VMEM((16, 1, 128), F32),
            pltpu.VMEM((4, 40, 128), F32),
            pltpu.VMEM((3, 40, 128), F32),
            pltpu.SemaphoreType.DMA((7,)),
            pltpu.SemaphoreType.DMA((sems,)),
            pltpu.SemaphoreType.DMA((sems,)),
        ],
        compiler_params=pltpu.CompilerParams(
            collective_id=0, has_side_effects=True, vmem_limit_bytes=24 * 1024 * 1024
        ),
        name="misfit_adjoint",
    )(*[pltpu.with_memory_space_constraint(a, pltpu.HBM) for a in (model, kern.reshape(2048, 256), observed, weights.reshape(1, 128))])
    gradient, misfit = pl.pallas_call(
        finish,
        out_shape=(jax.ShapeDtypeStruct((1, 16, 256), F32), jax.ShapeDtypeStruct((1, 1), F32)),
        in_specs=[pl.BlockSpec(memory_space=pltpu.VMEM)],
        out_specs=(pl.BlockSpec(memory_space=pltpu.VMEM), pl.BlockSpec(memory_space=pltpu.SMEM)),
        compiler_params=pltpu.CompilerParams(vmem_limit_bytes=4 * 1024 * 1024),
        name="finish",
    )(out)
    return gradient, misfit.reshape(())


def solution(mesh):
    nz = mesh.shape["par"] // (NX * NY)
    entries = 4 * 128 * mesh.shape["sens"] * 256
    return jax.shard_map(
        functools.partial(local, nz, 0.5 / entries),
        mesh=mesh,
        in_specs=(P("sens", "par", None), P("sens", "par", None), P(None, "sens", None), P("sens")),
        out_specs=(P("sens", "par", None), P()),
        check_vma=False,
    )
```

```python
import functools

import jax
import jax.numpy as jnp
from jax import lax
from jax.experimental import pallas as pl
from jax.experimental.pallas import tpu as pltpu
from jax.sharding import PartitionSpec as P

MESH = pl.DeviceIdType.MESH
F32 = jnp.float32
BF16 = jnp.bfloat16
NX = 4
NY = 4
B = 16
ORDER = (2, 1, 3)
PLANE = tuple((dx, dy) for dx in (2, 1, 3, 0) for dy in (2, 1, 3, 0) if dx or dy)


def nt(a, b):
    return lax.dot_general(a, b, (((1,), (1,)), ((), ())), preferred_element_type=F32)


def nn(a, b):
    return jnp.dot(a, b, preferred_element_type=F32)


def kernel(
    nz,
    scale,
    model_ref,
    kern_ref,
    obs_ref,
    weights_ref,
    out_ref,
    kv,
    kp,
    kt,
    w2,
    eye,
    swap,
    w_ref,
    mg,
    xp,
    ob,
    ot,
    sp,
    rs,
    zb,
    rf,
    rp,
    mr,
    gs,
    gr,
    lsem,
    ssem,
    rsem,
):
    g = lax.axis_index("sens")
    par = lax.axis_index("par")
    z = par // (NX * NY)
    x = (par // NY) % NX
    y = par % NY

    def at_sens(d):
        return {"sens": (g + d) % 4, "par": par}

    def at_plane(dx, dy):
        return {"sens": g, "par": (z * NX + (x + dx) % NX) * NY + (y + dy) % NY}

    def at_z(d):
        return {"sens": g, "par": (((z + d) % nz) * NX + x) * NY + y}

    counter = [0]
    pending = []

    def phase(copies=3):
        base = counter[0]
        counter[0] += copies
        return base

    def send(number, src, dst, to):
        c = pltpu.make_async_remote_copy(
            src_ref=src,
            dst_ref=dst,
            send_sem=ssem.at[number],
            recv_sem=rsem.at[number],
            device_id=to,
            device_id_type=MESH,
        )
        c.start()
        pending.append(c)
        return c

    own = pltpu.make_async_copy(model_ref.at[0], mg.at[g], lsem.at[4])
    own.start()
    loads = []
    for n in range(4):
        c = pltpu.make_async_copy(kern_ref.at[pl.ds(512 * n, 512)], kv.at[pl.ds(512 * n, 512)], lsem.at[n])
        c.start()
        loads.append(c)
    load = pltpu.make_async_copy(
        obs_ref.at[x, :, pl.ds(pl.multiple_of(128 * (y // 2), 128), 128)], ob, lsem.at[5]
    )
    load.start()
    wload = pltpu.make_async_copy(weights_ref, w_ref, lsem.at[6])
    wload.start()

    barrier = pltpu.get_barrier_semaphore()
    zs = tuple(range(1, nz))
    for d in zs:
        pl.semaphore_signal(barrier, inc=1, device_id=at_z(d), device_id_type=MESH)
    for dx, dy in PLANE:
        pl.semaphore_signal(barrier, inc=1, device_id=at_plane(dx, dy), device_id_type=MESH)
    for d in ORDER:
        pl.semaphore_signal(barrier, inc=1, device_id=at_sens(d), device_id_type=MESH)

    rows = lax.broadcasted_iota(jnp.int32, (256, 256), 0)
    cols = lax.broadcasted_iota(jnp.int32, (256, 256), 1)
    eye[...] = jnp.where(rows == cols, 1.0, 0.0).astype(BF16)
    swap[...] = jnp.where((rows % 16) * 16 + rows // 16 == cols, 1.0, 0.0).astype(BF16)

    def spread(n):
        loads[n].wait()
        for m in (2 * n, 2 * n + 1):
            out = nn(swap[...], kv[pl.ds(256 * m, 256), :]).astype(BF16)
            kp[:, pl.ds(16 * m, 16), :] = out.reshape(16, 16, 256)

    for n in range(2):
        spread(n)
    own.wait()
    pl.semaphore_wait(barrier, len(PLANE) + 3 + len(zs))
    ph = phase()
    gather = [send(ph + d - 1, mg.at[g], mg.at[g], at_sens(d)) for d in ORDER]

    for n in range(2, 4):
        spread(n)

    for q in range(8):
        out = nt(eye[...], kp[2 * q : 2 * q + 2].reshape(256, 256)).astype(BF16)
        kt[2 * q] = out[:, :128]
        kt[2 * q + 1] = out[:, 128:]
    for c in range(8):
        lo = kt[:, 32 * c : 32 * c + 16, :].reshape(256, 128)
        hi = kt[:, 32 * c + 16 : 32 * c + 32, :].reshape(256, 128)
        out = nn(swap[...], jnp.concatenate([lo, hi], axis=1)).astype(BF16)
        w2[c] = out

    lane = lax.broadcasted_iota(jnp.int32, (16, 256), 1)

    def shifts(v):
        m = mg[v].astype(F32)
        pieces = [m.astype(BF16)]
        for i in range(1, B):
            pieces.append(jnp.where(lane >= i, pltpu.roll(m, i, axis=1), 0.0).astype(BF16))
        xp[v] = nt(eye[...], jnp.concatenate(pieces, axis=0)).astype(BF16)

    shifts(g)
    for c in gather:
        c.wait_recv()
    for d in ORDER:
        shifts((g + d) % 4)

    def predict(v):
        blocks = [None] * 16
        for c in range(8):
            out = nn(xp[v, 0 : B * (16 - 2 * c), :], w2[c])
            for b in range(16 - 2 * c):
                for e in (0, 1):
                    t = b + 2 * c + e
                    if t < 16:
                        part = out[B * b : B * b + B, 128 * e : 128 * e + 128]
                        blocks[t] = part if blocks[t] is None else blocks[t] + part
        return jnp.concatenate(blocks, axis=0)

    def quarter(n):
        return pl.ds(pl.multiple_of(64 * n, 64), 64)

    pha = phase(len(PLANE))
    ina = {}
    for some in ((2, 1), (3, 0)):
        for dx in some:
            sp[dx] = predict((x + dx) % NX)
        for n, (px, dy) in enumerate(PLANE):
            if px in some:
                ina[px, dy] = send(pha + n, sp.at[px, quarter((y + dy) % NY)], rs.at[n], at_plane(px, dy))
    load.wait()
    wload.wait()
    ot[...] = ob[...].T

    block = sp[0, quarter(y), :]
    for first in (0, 4, 8, 12):
        group = range(first, min(first + 4, len(PLANE)))
        for n in group:
            ina[PLANE[n]].wait_recv()
        part = rs[first]
        for n in group[1:]:
            part = part + rs[n]
        block = block + part

    phz = phase()
    zb[z] = block
    inz = [send(phz + d - 1, zb.at[z], zb.at[z], at_z(d)) for d in zs]
    for c in inz:
        c.wait_recv()
    total = zb[0]
    for n in range(1, nz):
        total = total + zb[n]

    mismatch = total - ot[pl.ds(pl.multiple_of(64 * (y % 2), 64), 64), :]
    weighted = w_ref[...] * mismatch
    rf[x, quarter(y), :] = weighted.astype(BF16)
    phb = phase(len(PLANE))
    inb = {}
    for n, (dx, dy) in enumerate(PLANE):
        inb[dx, dy] = send(phb + n, rf.at[x, quarter(y)], rf.at[x, quarter(y)], at_plane(dx, dy))

    sq = jnp.sum((weighted * mismatch).reshape(8, 8, 128), axis=0)
    here = NY * x + y
    mr[here] = jnp.sum(sq, axis=0, keepdims=True)
    phm = phase(len(PLANE))
    inm = [send(phm + n, mr.at[here], mr.at[here], at_plane(dx, dy)) for n, (dx, dy) in enumerate(PLANE)]

    rp[256:272, :] = jnp.zeros((16, 128), F32)
    group = lax.broadcasted_iota(jnp.int32, (B, 128), 1) // B

    def adjoint(v):
        rp[0:256, :] = rf[v].astype(F32)
        lhs = jnp.concatenate([rp[i : i + 256, :].astype(BF16) for i in range(B)], axis=1)
        rhs = jnp.concatenate(
            [
                jnp.concatenate([w2[:, B * i : B * i + B, 0:128], w2[:, B * i : B * i + B, 128:256]], axis=0).reshape(
                    256, 128
                )
                for i in range(B)
            ],
            axis=1,
        )
        out = nt(lhs, rhs)
        t = [out[B * b : B * b + B, :128] for b in range(16)]
        for b in range(15):
            t[b] = t[b] + out[B * b + B : B * b + 2 * B, 128:]
        for half in (0, 1):
            packed = None
            for r in range(-7, 8):
                picked = jnp.zeros((B, 128), F32)
                for c in range(max(0, -r), 8):
                    if 0 <= 2 * c + r < 8:
                        picked = jnp.where(group == c, t[2 * (2 * c + r) + half], picked)
                if r:
                    picked = pltpu.roll(picked, (B * r) % 128, axis=1)
                packed = picked if packed is None else packed + picked
            gs[v, B * half : B * half + B, :] = packed

    for c in inb.values():
        c.wait_recv()
    for d in ORDER:
        adjoint((g + d) % 4)
    for c in inm:
        c.wait_recv()
    parts = [mr[n] for n in range(NX * NY)]
    while len(parts) > 1:
        parts = [parts[n] + parts[n + 1] for n in range(0, len(parts), 2)]
    sq = jnp.where(lax.broadcasted_iota(jnp.int32, (8, 128), 0) == 0, parts[0], 0.0)

    phg = phase()
    ing = {}
    for d in ORDER:
        v = (g + d) % 4
        gs[v, 32:40, :] = sq
        ing[d] = send(phg + d - 1, gs.at[v], gr.at[d - 1], at_sens(d))
    adjoint(g)
    for d in ORDER:
        ing[d].wait_recv()
    out_ref[0:32, :] = (gs[g, 0:32, :] + gr[0, 0:32]) + (gr[1, 0:32] + gr[2, 0:32])
    total = jnp.zeros((8, 128), F32)
    parts = [sq] + [gr[d - 1, 32:40] for d in (1, 2, 3)]
    for owner in range(4):
        for d in range(4):
            total = total + jnp.where((g + 4 - d) % 4 == owner, parts[d], 0.0)
    out_ref[32:40, :] = total * scale
    for c in pending:
        c.wait_send()


def finish(in_ref, grad_ref, mis_ref):
    series = in_ref[0:32, :].T
    for c in range(8):
        grad_ref[0, :, 32 * c : 32 * c + 32] = series[B * c : B * c + B, :]
    mis_ref[0, 0] = jnp.sum(in_ref[32:40, :])


def local(nz, scale, model, kern, observed, weights):
    sems = 54
    out = pl.pallas_call(
        functools.partial(kernel, nz, scale),
        out_shape=jax.ShapeDtypeStruct((40, 128), F32),
        in_specs=[pl.BlockSpec(memory_space=pltpu.HBM)] * 4,
        out_specs=pl.BlockSpec(memory_space=pltpu.VMEM),
        scratch_shapes=[
            pltpu.VMEM((2048, 256), BF16),
            pltpu.VMEM((16, 128, 256), BF16),
            pltpu.VMEM((16, 256, 128), BF16),
            pltpu.VMEM((8, 256, 256), BF16),
            pltpu.VMEM((256, 256), BF16),
            pltpu.VMEM((256, 256), BF16),
            pltpu.VMEM((1, 128), F32),
            pltpu.VMEM((4, 16, 256), BF16),
            pltpu.VMEM((4, 256, 256), BF16),
            pltpu.VMEM((128, 128), F32),
            pltpu.VMEM((128, 128), F32),
            pltpu.VMEM((4, 256, 128), F32),
            pltpu.VMEM((15, 64, 128), F32),
            pltpu.VMEM((nz, 64, 128), F32),
            pltpu.VMEM((4, 256, 128), BF16),
            pltpu.VMEM((272, 128), F32),
            pltpu.VMEM((16, 1, 128), F32),
            pltpu.VMEM((4, 40, 128), F32),
            pltpu.VMEM((3, 40, 128), F32),
            pltpu.SemaphoreType.DMA((7,)),
            pltpu.SemaphoreType.DMA((sems,)),
            pltpu.SemaphoreType.DMA((sems,)),
        ],
        compiler_params=pltpu.CompilerParams(
            collective_id=0, has_side_effects=True, vmem_limit_bytes=24 * 1024 * 1024
        ),
        name="misfit_adjoint",
    )(*[pltpu.with_memory_space_constraint(a, pltpu.HBM) for a in (model, kern.reshape(2048, 256), observed, weights.reshape(1, 128))])
    gradient, misfit = pl.pallas_call(
        finish,
        out_shape=(jax.ShapeDtypeStruct((1, 16, 256), F32), jax.ShapeDtypeStruct((1, 1), F32)),
        in_specs=[pl.BlockSpec(memory_space=pltpu.VMEM)],
        out_specs=(pl.BlockSpec(memory_space=pltpu.VMEM), pl.BlockSpec(memory_space=pltpu.SMEM)),
        compiler_params=pltpu.CompilerParams(vmem_limit_bytes=4 * 1024 * 1024),
        name="finish",
    )(out)
    return gradient, misfit.reshape(())


def solution(mesh):
    nz = mesh.shape["par"] // (NX * NY)
    entries = 4 * 128 * mesh.shape["sens"] * 256
    return jax.shard_map(
        functools.partial(local, nz, 0.5 / entries),
        mesh=mesh,
        in_specs=(P("sens", "par", None), P("sens", "par", None), P(None, "sens", None), P("sens")),
        out_specs=(P("sens", "par", None), P()),
        check_vma=False,
    )
```

```python
import functools

import jax
import jax.numpy as jnp
from jax import lax
from jax.experimental import pallas as pl
from jax.experimental.pallas import tpu as pltpu
from jax.sharding import PartitionSpec as P

MESH = pl.DeviceIdType.MESH
F32 = jnp.float32
BF16 = jnp.bfloat16
NX = 4
NY = 4
B = 16
ORDER = (2, 1, 3)
PLANE = tuple((dx, dy) for dx in (2, 1, 3, 0) for dy in (2, 1, 3, 0) if dx or dy)


def nt(a, b):
    return lax.dot_general(a, b, (((1,), (1,)), ((), ())), preferred_element_type=F32)


def nn(a, b):
    return jnp.dot(a, b, preferred_element_type=F32)


def kernel(
    nz,
    scale,
    model_ref,
    kern_ref,
    obs_ref,
    weights_ref,
    out_ref,
    kv,
    kp,
    kt,
    w2,
    eye,
    swap,
    w_ref,
    mg,
    xp,
    ob,
    ot,
    sp,
    rs,
    zb,
    rf,
    rp,
    mr,
    gs,
    gr,
    lsem,
    ssem,
    rsem,
):
    g = lax.axis_index("sens")
    par = lax.axis_index("par")
    z = par // (NX * NY)
    x = (par // NY) % NX
    y = par % NY

    def at_sens(d):
        return {"sens": (g + d) % 4, "par": par}

    def at_plane(dx, dy):
        return {"sens": g, "par": (z * NX + (x + dx) % NX) * NY + (y + dy) % NY}

    def at_z(d):
        return {"sens": g, "par": (((z + d) % nz) * NX + x) * NY + y}

    counter = [0]
    pending = []

    def phase(copies=3):
        base = counter[0]
        counter[0] += copies
        return base

    def send(number, src, dst, to):
        c = pltpu.make_async_remote_copy(
            src_ref=src,
            dst_ref=dst,
            send_sem=ssem.at[number],
            recv_sem=rsem.at[number],
            device_id=to,
            device_id_type=MESH,
        )
        c.start()
        pending.append(c)
        return c

    own = pltpu.make_async_copy(model_ref.at[0], mg.at[g], lsem.at[4])
    own.start()
    loads = []
    for n in range(4):
        c = pltpu.make_async_copy(kern_ref.at[pl.ds(512 * n, 512)], kv.at[pl.ds(512 * n, 512)], lsem.at[n])
        c.start()
        loads.append(c)
    load = pltpu.make_async_copy(
        obs_ref.at[x, :, pl.ds(pl.multiple_of(128 * (y // 2), 128), 128)], ob, lsem.at[5]
    )
    load.start()
    wload = pltpu.make_async_copy(weights_ref, w_ref, lsem.at[6])
    wload.start()

    barrier = pltpu.get_barrier_semaphore()
    zs = tuple(range(1, nz))
    for d in zs:
        pl.semaphore_signal(barrier, inc=1, device_id=at_z(d), device_id_type=MESH)
    for dx, dy in PLANE:
        pl.semaphore_signal(barrier, inc=1, device_id=at_plane(dx, dy), device_id_type=MESH)
    for d in ORDER:
        pl.semaphore_signal(barrier, inc=1, device_id=at_sens(d), device_id_type=MESH)

    rows = lax.broadcasted_iota(jnp.int32, (256, 256), 0)
    cols = lax.broadcasted_iota(jnp.int32, (256, 256), 1)
    eye[...] = jnp.where(rows == cols, 1.0, 0.0).astype(BF16)
    swap[...] = jnp.where((rows % 16) * 16 + rows // 16 == cols, 1.0, 0.0).astype(BF16)

    def spread(n):
        loads[n].wait()
        for m in (2 * n, 2 * n + 1):
            out = nn(swap[...], kv[pl.ds(256 * m, 256), :]).astype(BF16)
            kp[:, pl.ds(16 * m, 16), :] = out.reshape(16, 16, 256)

    for n in range(2):
        spread(n)
    own.wait()
    pl.semaphore_wait(barrier, len(PLANE) + 3 + len(zs))
    ph = phase()
    gather = [send(ph + d - 1, mg.at[g], mg.at[g], at_sens(d)) for d in ORDER]

    for n in range(2, 4):
        spread(n)

    for q in range(8):
        out = nt(eye[...], kp[2 * q : 2 * q + 2].reshape(256, 256)).astype(BF16)
        kt[2 * q] = out[:, :128]
        kt[2 * q + 1] = out[:, 128:]
    for c in range(8):
        lo = kt[:, 32 * c : 32 * c + 16, :].reshape(256, 128)
        hi = kt[:, 32 * c + 16 : 32 * c + 32, :].reshape(256, 128)
        out = nn(swap[...], jnp.concatenate([lo, hi], axis=1)).astype(BF16)
        w2[c] = out

    lane = lax.broadcasted_iota(jnp.int32, (16, 256), 1)

    def shifts(v):
        m = mg[v].astype(F32)
        pieces = [m.astype(BF16)]
        for i in range(1, B):
            pieces.append(jnp.where(lane >= i, pltpu.roll(m, i, axis=1), 0.0).astype(BF16))
        xp[v] = nt(eye[...], jnp.concatenate(pieces, axis=0)).astype(BF16)

    shifts(g)
    for c in gather:
        c.wait_recv()
    for d in ORDER:
        shifts((g + d) % 4)

    def predict(v):
        blocks = [None] * 16
        for c in range(8):
            out = nn(xp[v, 0 : B * (16 - 2 * c), :], w2[c])
            for b in range(16 - 2 * c):
                for e in (0, 1):
                    t = b + 2 * c + e
                    if t < 16:
                        part = out[B * b : B * b + B, 128 * e : 128 * e + 128]
                        blocks[t] = part if blocks[t] is None else blocks[t] + part
        return jnp.concatenate(blocks, axis=0)

    def half(n, h):
        return pl.ds(pl.multiple_of(64 * n + 32 * h, 32), 32)

    copies = len(PLANE)
    pha = phase(2 * copies)
    ina = {}

    def scatter(h, some):
        for n, (dx, dy) in enumerate(PLANE):
            if dx in some:
                ina[h, n] = send(
                    pha + copies * h + n,
                    sp.at[dx, half((y + dy) % NY, h)],
                    rs.at[copies * h + n],
                    at_plane(dx, dy),
                )

    for some in ((2, 1), (3, 0)):
        for dx in some:
            sp[dx] = predict((x + dx) % NX)
        scatter(0, some)
    scatter(1, (2, 1))
    scatter(1, (3, 0))

    load.wait()
    wload.wait()
    ot[...] = ob[...].T

    phz = phase(6)
    inz = []
    for h in (0, 1):
        for n in range(copies):
            ina[h, n].wait_recv()
        parts = [sp[0, half(y, h), :]] + [rs[copies * h + n] for n in range(copies)]
        while len(parts) > 1:
            parts = [parts[n] + parts[n + 1] for n in range(0, len(parts), 2)]
        zb[h, z] = parts[0]
        inz.append([send(phz + 3 * h + d - 1, zb.at[h, z], zb.at[h, z], at_z(d)) for d in zs])

    phb = phase(2 * copies)
    inb = []
    squares = []
    for h in (0, 1):
        for c in inz[h]:
            c.wait_recv()
        total = zb[h, 0]
        for n in range(1, nz):
            total = total + zb[h, n]
        mismatch = total - ot[half(y % 2, h), :]
        weighted = w_ref[...] * mismatch
        rf[x, half(y, h), :] = weighted.astype(BF16)
        for n, (dx, dy) in enumerate(PLANE):
            mine = rf.at[x, half(y, h)]
            inb.append(send(phb + copies * h + n, mine, mine, at_plane(dx, dy)))
        squares.append(jnp.sum((weighted * mismatch).reshape(4, 8, 128), axis=0))

    sq = squares[0] + squares[1]
    here = NY * x + y
    mr[here] = jnp.sum(sq, axis=0, keepdims=True)
    phm = phase(len(PLANE))
    inm = [send(phm + n, mr.at[here], mr.at[here], at_plane(dx, dy)) for n, (dx, dy) in enumerate(PLANE)]

    rp[256:272, :] = jnp.zeros((16, 128), F32)
    group = lax.broadcasted_iota(jnp.int32, (B, 128), 1) // B

    def adjoint(v):
        rp[0:256, :] = rf[v].astype(F32)
        lhs = jnp.concatenate([rp[i : i + 256, :].astype(BF16) for i in range(B)], axis=1)
        rhs = jnp.concatenate(
            [
                jnp.concatenate([w2[:, B * i : B * i + B, 0:128], w2[:, B * i : B * i + B, 128:256]], axis=0).reshape(
                    256, 128
                )
                for i in range(B)
            ],
            axis=1,
        )
        out = nt(lhs, rhs)
        t = [out[B * b : B * b + B, :128] for b in range(16)]
        for b in range(15):
            t[b] = t[b] + out[B * b + B : B * b + 2 * B, 128:]
        for half in (0, 1):
            packed = None
            for r in range(-7, 8):
                picked = jnp.zeros((B, 128), F32)
                for c in range(max(0, -r), 8):
                    if 0 <= 2 * c + r < 8:
                        picked = jnp.where(group == c, t[2 * (2 * c + r) + half], picked)
                if r:
                    picked = pltpu.roll(picked, (B * r) % 128, axis=1)
                packed = picked if packed is None else packed + picked
            gs[v, B * half : B * half + B, :] = packed

    for c in inb:
        c.wait_recv()
    for d in ORDER:
        adjoint((g + d) % 4)
    for c in inm:
        c.wait_recv()
    parts = [mr[n] for n in range(NX * NY)]
    while len(parts) > 1:
        parts = [parts[n] + parts[n + 1] for n in range(0, len(parts), 2)]
    sq = jnp.where(lax.broadcasted_iota(jnp.int32, (8, 128), 0) == 0, parts[0], 0.0)

    phg = phase()
    ing = {}
    for d in ORDER:
        v = (g + d) % 4
        gs[v, 32:40, :] = sq
        ing[d] = send(phg + d - 1, gs.at[v], gr.at[d - 1], at_sens(d))
    adjoint(g)
    for d in ORDER:
        ing[d].wait_recv()
    out_ref[0:32, :] = (gs[g, 0:32, :] + gr[0, 0:32]) + (gr[1, 0:32] + gr[2, 0:32])
    total = jnp.zeros((8, 128), F32)
    parts = [sq] + [gr[d - 1, 32:40] for d in (1, 2, 3)]
    for owner in range(4):
        for d in range(4):
            total = total + jnp.where((g + 4 - d) % 4 == owner, parts[d], 0.0)
    out_ref[32:40, :] = total * scale
    for c in pending:
        c.wait_send()


def finish(in_ref, grad_ref, mis_ref):
    series = in_ref[0:32, :].T
    for c in range(8):
        grad_ref[0, :, 32 * c : 32 * c + 32] = series[B * c : B * c + B, :]
    mis_ref[0, 0] = jnp.sum(in_ref[32:40, :])


def local(nz, scale, model, kern, observed, weights):
    sems = 87
    out = pl.pallas_call(
        functools.partial(kernel, nz, scale),
        out_shape=jax.ShapeDtypeStruct((40, 128), F32),
        in_specs=[pl.BlockSpec(memory_space=pltpu.HBM)] * 4,
        out_specs=pl.BlockSpec(memory_space=pltpu.VMEM),
        scratch_shapes=[
            pltpu.VMEM((2048, 256), BF16),
            pltpu.VMEM((16, 128, 256), BF16),
            pltpu.VMEM((16, 256, 128), BF16),
            pltpu.VMEM((8, 256, 256), BF16),
            pltpu.VMEM((256, 256), BF16),
            pltpu.VMEM((256, 256), BF16),
            pltpu.VMEM((1, 128), F32),
            pltpu.VMEM((4, 16, 256), BF16),
            pltpu.VMEM((4, 256, 256), BF16),
            pltpu.VMEM((128, 128), F32),
            pltpu.VMEM((128, 128), F32),
            pltpu.VMEM((4, 256, 128), F32),
            pltpu.VMEM((30, 32, 128), F32),
            pltpu.VMEM((2, nz, 32, 128), F32),
            pltpu.VMEM((4, 256, 128), BF16),
            pltpu.VMEM((272, 128), F32),
            pltpu.VMEM((16, 1, 128), F32),
            pltpu.VMEM((4, 40, 128), F32),
            pltpu.VMEM((3, 40, 128), F32),
            pltpu.SemaphoreType.DMA((7,)),
            pltpu.SemaphoreType.DMA((sems,)),
            pltpu.SemaphoreType.DMA((sems,)),
        ],
        compiler_params=pltpu.CompilerParams(
            collective_id=0, has_side_effects=True, vmem_limit_bytes=24 * 1024 * 1024
        ),
        name="misfit_adjoint",
    )(*[pltpu.with_memory_space_constraint(a, pltpu.HBM) for a in (model, kern.reshape(2048, 256), observed, weights.reshape(1, 128))])
    gradient, misfit = pl.pallas_call(
        finish,
        out_shape=(jax.ShapeDtypeStruct((1, 16, 256), F32), jax.ShapeDtypeStruct((1, 1), F32)),
        in_specs=[pl.BlockSpec(memory_space=pltpu.VMEM)],
        out_specs=(pl.BlockSpec(memory_space=pltpu.VMEM), pl.BlockSpec(memory_space=pltpu.SMEM)),
        compiler_params=pltpu.CompilerParams(vmem_limit_bytes=4 * 1024 * 1024),
        name="finish",
    )(out)
    return gradient, misfit.reshape(())


def solution(mesh):
    nz = mesh.shape["par"] // (NX * NY)
    entries = 4 * 128 * mesh.shape["sens"] * 256
    return jax.shard_map(
        functools.partial(local, nz, 0.5 / entries),
        mesh=mesh,
        in_specs=(P("sens", "par", None), P("sens", "par", None), P(None, "sens", None), P("sens")),
        out_specs=(P("sens", "par", None), P()),
        check_vma=False,
    )
```
